32 devices in a mesh: groups: 2 (over x), src: 8 (over z, y), tile: 2 (over core).
Axes of the slice: x: 2, y: 2, z: 4, core: 2. Of those that a mesh axis runs over, the one named last changes fastest.
Arguments:
- mask: float32 [2048, 1024], P(('groups', 'tile')), parts along dimension 0, may hold values from 0 to 1
- target: float32 [2048, 1024], P(('groups', 'tile')), parts along dimension 0, may hold values from 0 to 1
- pupil: float32 [64, 64], replicated, may hold values from 0.1 to 1.9
- source_shift: int32 [24, 2], replicated, may hold values from -24 to 24
- source_weight: float32 [24], replicated, may hold values from 0.25 to 4
Outputs:
- mask_gradient: float32 [2048, 1024], P(('groups', 'tile'), 'src'), parts along dimension 0
The draws below stay inside these ranges and needn't reach their ends.
There are 2 independent parts, one for each index of `groups`. The reference program is written for one: setup_inputs(seed, part) draws one part's arguments, and reference() takes and returns one part's arrays. A program takes and returns all parts, laid end to end along the dimension named above; an argument that names none is the same for every part. Nothing has to cross between parts.
Inputs may be any that keep to these rules, and one draw needn't show every extreme that they name: `source_shift`: integer frequency shifts of the source points.
All inputs are finite; a program needn't handle non-finite values.
Results may differ from the reference program's by a relative error of at most 0.0003.
Values sent between devices are 32-bit elements; how exact they have to be, the bound alone decides.
A program may use at most 128 MiB of HBM per device.

```python
import math
import jax
import jax.numpy as jnp
from jax import lax

TS = 512
HALO = 64
K = 64
SRC_DEV = 3
GC = 2
PAD = 640
SOURCES = 24
ROWS = 1024
COLS = 1024
N_SRC = 8
N_TILE = 2


def place_ends(array, key, smallest, high):
    extent = array.shape
    index_at = [jax.random.randint(jax.random.fold_in(key, axis), (), 0, extent[axis]) for axis in range(len(extent))]
    array = array.at[tuple(index_at)].set(smallest)
    longest = extent.index(max(extent))
    index_at[longest] = (index_at[longest] + 1) % extent[longest]
    return array.at[tuple(index_at)].set(high)


def steps_of(own_key, extent, shards, low, largest):
    loudness = 1.0
    for axis_at, blocks in shards:
        draws = jax.random.uniform(jax.random.fold_in(jax.random.fold_in(own_key, 6), axis_at), (blocks,), jnp.float32, low / len(shards), largest / len(shards))
        loudness = loudness * jnp.repeat(jnp.exp(draws), extent[axis_at] // blocks).reshape((-1,) + (1,) * (len(extent) - 1 - axis_at))
    return loudness


def setup_inputs(seed: int = 0, part: int = 0) -> dict:
    splits = jax.random.split(jax.random.key(seed), 6)
    part_keys = jax.random.split(jax.random.fold_in(splits[5], part), 6)
    mask = jnp.clip(1.0 * jax.random.uniform(part_keys[0], (ROWS, COLS), jnp.float32) ** steps_of(part_keys[0], (ROWS, COLS), ((0, 2),), -0.2, 0.2), 0.0, 1.0)
    target = jnp.clip(1.0 * jax.random.uniform(part_keys[1], (ROWS, COLS), jnp.float32) ** steps_of(part_keys[1], (ROWS, COLS), ((0, 2),), -0.2, 0.2), 0.0, 1.0)
    pupil = jnp.clip(1.0 + 0.18 * jax.random.normal(splits[2], (K, K), jnp.float32), 0.1, 1.9)
    source_shift = place_ends(jax.random.randint(splits[3], (SOURCES, 2), -((3 * K) // 8), (3 * K) // 8 + 1), jax.random.fold_in(splits[3], 1), -((3 * K) // 8), ((3 * K) // 8 + 1) - 1).astype(jnp.int32)
    source_weight = jnp.clip(jnp.exp(jax.random.uniform(splits[4], (SOURCES,), jnp.float32, math.log(0.25), math.log(4.0))), 0.25, 4.0)
    return dict(mask=mask, target=target, pupil=pupil, source_shift=source_shift, source_weight=source_weight)


full_turn = 2.0 * math.pi
exact_mode = lax.Precision.HIGHEST
resist_gain = 25.0
resist_level = 0.25

def light_block(tiles, shift_block, weight_block, pupil):
    sources = shift_block.shape[0]
    freqs = pupil.shape[0]
    padded = tiles.shape[1]
    count = tiles.shape[0]
    scaling = full_turn / padded
    centred = jnp.arange(freqs, dtype=jnp.int32) - freqs // 2
    pixels = jnp.arange(padded, dtype=jnp.int32)
    row_freq = centred[None, :] + shift_block[:, 0:1]
    col_freq = centred[None, :] + shift_block[:, 1:2]
    row_phase = jnp.mod(row_freq[:, :, None] * pixels[None, None, :], padded).astype(jnp.float32) * scaling
    col_phase = jnp.mod(col_freq[:, :, None] * pixels[None, None, :], padded).astype(jnp.float32) * scaling
    col_table = jnp.concatenate([jnp.cos(col_phase), -jnp.sin(col_phase)], axis=1)
    col_table = col_table.reshape(sources * 2 * freqs, padded).T
    halfway = jnp.einsum('gxy,yn->gxn', tiles, col_table, precision=exact_mode)
    halfway = halfway.reshape(count, padded, sources, 2 * freqs)
    row_table = jnp.concatenate([jnp.cos(row_phase), jnp.sin(row_phase)], axis=1)
    products = jnp.einsum('sux,gxsn->gsun', row_table, halfway, precision=exact_mode)
    spec_real = (products[:, :, :freqs, :freqs] + products[:, :, freqs:, freqs:]) * pupil
    spec_imag = (products[:, :, :freqs, freqs:] - products[:, :, freqs:, :freqs]) * pupil
    outputs = jnp.arange(TS, dtype=jnp.int32) + HALO
    out_phase = jnp.mod(outputs[:, None] * centred[None, :], padded).astype(jnp.float32) * scaling
    back_cos = jnp.cos(out_phase) / padded
    back_sin = jnp.sin(out_phase) / padded
    back_stack = jnp.concatenate([back_cos, back_sin], axis=0)
    spectra = jnp.concatenate([spec_real, spec_imag], axis=-1)
    mixed = jnp.einsum('xu,gsun->gsxn', back_stack, spectra, precision=exact_mode)
    left_real = mixed[:, :, :TS, :freqs] - mixed[:, :, TS:, freqs:]
    left_imag = mixed[:, :, :TS, freqs:] + mixed[:, :, TS:, :freqs]
    rows_both = jnp.concatenate([left_real, left_imag], axis=-1)
    upper_half = jnp.concatenate([back_cos.T, back_sin.T], axis=1)
    lower_half = jnp.concatenate([-back_sin.T, back_cos.T], axis=1)
    right_table = jnp.concatenate([upper_half, lower_half], axis=0)
    field = jnp.einsum('gsxk,kn->gsxn', rows_both, right_table, precision=exact_mode)
    power = field[..., :TS] * field[..., :TS] + field[..., TS:] * field[..., TS:]
    return lax.optimization_barrier(jnp.sum(power * weight_block[None, :, None, None], axis=1))

def resist_slope(intensity, target):
    printed = jax.nn.sigmoid(resist_gain * (intensity - resist_level))
    return 2.0 * (printed - target) * resist_gain * printed * (1.0 - printed)

def tile_stack(mask_image):
    widened = jnp.pad(mask_image, HALO)
    pieces = []
    for tile_row in range(N_TILE):
        for tile_column in range(GC):
            pieces.append(widened[tile_row * TS:tile_row * TS + PAD, tile_column * TS:tile_column * TS + PAD])
    return jnp.stack(pieces)

def to_image(tiles):
    return tiles.reshape(N_TILE, GC, TS, TS).transpose(0, 2, 1, 3).reshape(N_TILE * TS, GC * TS)

def from_image(image):
    return image.reshape(N_TILE, TS, GC, TS).transpose(0, 2, 1, 3).reshape(N_TILE * GC, TS, TS)

def reference(mask, target, pupil, source_shift, source_weight):
    tiles, unstack = jax.vjp(tile_stack, mask)
    shift_blocks = source_shift.reshape(N_SRC, SRC_DEV, 2)
    weight_blocks = source_weight.reshape(N_SRC, SRC_DEV)
    total_weight = jnp.sum(source_weight)

    def forward_step(carry, block):
        return (carry + light_block(tiles, block[0], block[1], pupil), None)
    start = jnp.zeros((N_TILE * GC, TS, TS), jnp.float32)
    summed, _ = lax.scan(forward_step, start, (shift_blocks, weight_blocks))
    intensity = to_image(summed) / total_weight
    slope_tiles = from_image(resist_slope(intensity, target) / total_weight)

    def backward_step(carry, block):

        def local_light(tile_input):
            return light_block(tile_input, block[0], block[1], pupil)
        _, pullback = jax.vjp(local_light, tiles)
        return (carry + pullback(slope_tiles)[0], None)
    gathered, _ = lax.scan(backward_step, jnp.zeros_like(tiles), (shift_blocks, weight_blocks))
    return unstack(gathered)[0]
```

```python
import functools

import numpy as np

import jax
import jax.numpy as jnp
from jax import lax
from jax.experimental import pallas as pl
from jax.experimental.pallas import tpu as pltpu
from jax.sharding import PartitionSpec as P

TS = 512
HALO = 64
PAD = 640
GRID = 128
REACH = 24
HALF = GRID // 2
CHUNK = 128
BLOCK = 4

MESH = pl.DeviceIdType.MESH
f32, bf16 = jnp.float32, jnp.bfloat16
resist_gain = 25.0
resist_level = 0.25

NN = (((1,), (0,)), ((), ()))
NT = (((1,), (1,)), ((), ()))


def two(array):
    high = array.astype(np.float32).astype(bf16)
    low = (array - high.astype(np.float64)).astype(bf16)
    return np.stack([high, low])


def tables(freqs):
    turn_of = 2.0 * np.pi / PAD
    reach = freqs // 2 + REACH
    frame = np.zeros(GRID)
    frame[: 2 * reach] = np.arange(-reach, reach)
    inside = np.zeros(GRID)
    inside[: 2 * reach] = 1.0

    columns = np.arange(-HALO, PAD + HALO)
    angle = turn_of * ((columns[:, None] * frame[None, :].astype(int)) % PAD)
    valid = ((columns >= 0) & (columns < PAD))[:, None] * inside[None, :]
    across = np.concatenate([np.cos(angle) * valid, np.sin(angle) * valid], axis=1)

    rows = np.arange(PAD)
    k = np.arange(HALF)
    used = (k <= reach)[:, None]
    angle = turn_of * ((k[:, None] * rows[None, :]) % PAD)
    down = np.concatenate([np.cos(angle) * used, -np.sin(angle) * used], axis=0)

    points = np.arange(GRID)
    angle = 2.0 * np.pi / GRID * ((frame[:, None].astype(int) * points[None, :]) % GRID)
    cosine, sine = np.cos(angle) * inside[:, None], np.sin(angle) * inside[:, None]
    wave = np.block([[cosine, sine], [-sine, cosine]])

    centre = np.arange(-freqs // 2, freqs // 2)
    angle = 2.0 * np.pi / GRID * ((points[:, None] * centre[None, :]) % GRID)
    turn = np.block([[np.cos(angle), -np.sin(angle)], [np.sin(angle), np.cos(angle)]])

    samples = points * (PAD // GRID)
    spread = np.ones((PAD, GRID))
    for p in range(1, GRID // 2):
        spread += 2.0 * np.cos(2.0 * np.pi * (p * (rows[:, None] - samples[None, :]) % PAD) / PAD)
    core = (spread / GRID)[HALO : HALO + TS]
    return across, down, wave, turn, core


def split(x):
    high = x.astype(bf16)
    return high, (x - high.astype(f32)).astype(bf16)


def dot(a, b, dims=NN):
    return lax.dot_general(a, b, dims, preferred_element_type=f32)


def mm(a, b, dims=NN):
    return dot(a[0], b[0], dims) + (dot(a[0], b[1], dims) + dot(a[1], b[0], dims))


def pair(ref, *index):
    return ref[(0, *index)], ref[(1, *index)]


def each(count, body):
    if count <= 8:
        for i in range(count):
            body(i)
    else:
        lax.fori_loop(0, count, lambda i, c: (body(i), c)[1], 0)


def at(i, size):
    start = i * size
    return pl.ds(start if isinstance(start, int) else pl.multiple_of(start, size), size)


def kernel(
    n, tiles, sources, freqs, overlap, hop,
    mask_any, target_any, pupil_ref, shift_ref, weight_ref,
    across_any, down_any, downt_any, near_any, neart_any, wave_any, wavet_any, turn_any, turnt_any, core_any, coret_any,
    out_ref,
    across_ref, down_ref, downt_ref, near_ref, neart_ref, wave_ref, wavet_ref, turn_ref, turnt_ref, core_ref, coret_ref,
    mask_ref, target_ref, halo_ref, lens_ref, pick_ref, place_ref, field_ref, light_ref, pull_ref, back_ref,
    own_ref, other_ref, give_ref, side_ref, corner_ref,
    load_sem, halo_sem, own_sem, give_sem, side_sem,
):
    me = lax.axis_index("src")
    side = lax.axis_index("tile")
    per = n // tiles
    c = me // per
    width = out_ref.shape[1]
    counted = HALO // overlap
    edge = me - per
    lefts = (edge >= -counted) & (edge < 0)
    rights = (edge >= 0) & (edge < counted)
    needs = lefts | rights
    source = jnp.where(edge < 0, me + hop, me - hop)
    gives = ((edge - hop >= -counted) & (edge - hop < 0)) | ((edge + hop >= 0) & (edge + hop < counted))
    taker = jnp.where(edge < 0, me + hop, me - hop)

    barrier = pltpu.get_barrier_semaphore()
    side_ref[...] = jnp.zeros_like(side_ref)
    corner_ref[...] = jnp.zeros_like(corner_ref)
    pl.semaphore_signal(barrier, inc=1, device_id={"tile": 1 - side}, device_id_type=MESH)

    @pl.when(needs)
    def _():
        for core in (0, 1):
            pl.semaphore_signal(barrier, inc=1, device_id={"src": source, "tile": core}, device_id_type=MESH)

    first = pl.multiple_of((TS - HALO) * (1 - side), HALO)
    start = pl.multiple_of(c * (mask_any.shape[1] - PAD), GRID)
    begin = pl.multiple_of(c * TS, GRID)
    places = [
        (mask_any.at[:, pl.ds(start, PAD)], mask_ref), (down_any, down_ref), (near_any.at[side], near_ref),
        (across_any.at[:, pl.ds(pl.multiple_of((1 - c) * 2 * HALO, GRID), PAD)], across_ref),
        (wave_any, wave_ref), (turn_any, turn_ref), (core_any, core_ref), (coret_any, coret_ref),
        (target_any.at[:, pl.ds(begin, TS)], target_ref), (turnt_any, turnt_ref), (wavet_any, wavet_ref),
        (downt_any, downt_ref), (neart_any.at[1 - side], neart_ref),
    ]
    loads = [pltpu.make_async_copy(a, b, load_sem.at[i]) for i, (a, b) in enumerate(places)]
    for load in loads:
        load.start()

    scaled = jnp.concatenate([pupil_ref[...] * (1.0 / (PAD * PAD)), jnp.zeros((freqs, GRID - freqs), f32)], axis=1)

    def lens(s):
        lens_ref[at(s, freqs)] = pltpu.roll(scaled, shift_ref[1, s] + REACH, axis=1)
        w = lax.broadcasted_iota(jnp.int32, (freqs, GRID), 0) + (shift_ref[0, s] - freqs // 2)
        lane = lax.broadcasted_iota(jnp.int32, (freqs, GRID), 1)
        cosine = (lane == jnp.abs(w)).astype(f32)
        sine = ((lane - HALF == w) & (w > 0)).astype(f32) - ((lane - HALF == -w) & (w < 0)).astype(f32)
        both = (cosine + sine).astype(bf16)
        pick_ref[at(s, freqs)] = jnp.concatenate([both, both], axis=1)

    each(sources, lens)

    group = GRID // freqs

    def places_of(i):
        lane = lax.broadcasted_iota(jnp.int32, (GRID, GRID), 1)
        row = lax.broadcasted_iota(jnp.int32, (GRID, GRID), 0)
        w = lane - freqs // 2 + shift_ref[0, i * group]
        for g in range(1, group):
            w = jnp.where(lane >= g * freqs, lane - g * freqs - freqs // 2 + shift_ref[0, i * group + g], w)
        cosine = (row == jnp.abs(w)).astype(f32)
        sine = ((row - HALF == w) & (w > 0)).astype(f32) - ((row - HALF == -w) & (w < 0)).astype(f32)
        place_ref[:, at(i, GRID)] = (cosine + sine).astype(bf16)

    each(sources // group, places_of)

    weight = weight_ref[0]
    for s in range(1, sources):
        weight = weight + weight_ref[s]
    inverse = 1.0 / jnp.full((1, GRID), weight, f32)

    pl.semaphore_wait(barrier, 1 + 2 * gives.astype(jnp.int32))
    halo = pltpu.make_async_remote_copy(
        src_ref=mask_any.at[pl.ds(first, HALO), pl.ds(start, PAD)],
        dst_ref=halo_ref,
        send_sem=halo_sem.at[0],
        recv_sem=halo_sem.at[1],
        device_id={"tile": 1 - side},
        device_id_type=MESH,
    )
    halo.start()

    for load in loads[:3]:
        load.wait()
    rows = mm(pair(down_ref), split(mask_ref[...]))
    halo.wait_recv()
    rows = rows + mm(pair(near_ref), split(halo_ref[...]))
    loads[3].wait()
    low = mm(split(rows), pair(across_ref))
    spectrum = split(
        jnp.concatenate(
            [
                jnp.concatenate([low[:HALF, :GRID], -low[:HALF, GRID:]], axis=1),
                jnp.concatenate([low[HALF:, GRID:], low[HALF:, :GRID]], axis=1),
            ],
            axis=0,
        )
    )
    spectrum = jnp.concatenate(spectrum, axis=0)

    for load in loads[4:6]:
        load.wait()
    light_ref[...] = jnp.zeros_like(light_ref)
    wave = pair(wave_ref)
    turn = turn_ref[...]

    def image(i):
        window = dot(pick_ref[at(i, BLOCK * freqs)], spectrum)
        lenses = lens_ref[at(i, BLOCK * freqs)]
        spec = split(window * jnp.concatenate([lenses, lenses], axis=1))
        z = mm(spec, wave)
        stack = jnp.concatenate(
            [
                jnp.concatenate([z[s * freqs : (s + 1) * freqs, :GRID], z[s * freqs : (s + 1) * freqs, GRID:]], axis=0)
                for s in range(BLOCK)
            ],
            axis=1,
        )
        high, less = split(stack)
        field = dot(turn, jnp.concatenate([high, high, less], axis=0))
        field_ref[:, at(i, BLOCK * GRID)] = field
        light = light_ref[...]
        for s in range(BLOCK):
            re = field[:GRID, s * GRID : (s + 1) * GRID]
            im = field[GRID:, s * GRID : (s + 1) * GRID]
            light = light + weight_ref[i * BLOCK + s] * (re * re + im * im)
        light_ref[...] = light

    each(sources // BLOCK, image)

    for load in loads[6:9]:
        load.wait()
    core = pair(core_ref)
    coret = pair(coret_ref)
    up = mm(core, split(light_ref[...] * (resist_gain * inverse)))
    pull = jnp.zeros((GRID, GRID), f32)
    for i in range(TS // CHUNK):
        part = slice(i * CHUNK, (i + 1) * CHUNK)
        fine = mm(split(up[part]), coret)
        decay = jnp.exp(resist_gain * resist_level - fine)
        printed = 1.0 / (1.0 + decay)
        slope = (printed - target_ref[part]) * (decay * printed * printed)
        pull = pull + mm(pair(coret_ref, slice(None), part), split(mm(split(slope), core)))
    pull = pull * (2.0 * resist_gain * inverse)
    pull = jnp.concatenate([pull, pull], axis=0)

    for load in loads[9:]:
        load.wait()
    turnt = pair(turnt_ref)
    wavet = pair(wavet_ref)
    back_ref[...] = jnp.zeros_like(back_ref)

    def gradient(i):
        field = field_ref[:, at(i, BLOCK * GRID)]
        u = mm(turnt, split(field * jnp.concatenate([pull] * BLOCK, axis=1)))
        stack = jnp.concatenate(
            [
                jnp.concatenate([u[:freqs, s * GRID : (s + 1) * GRID], u[freqs:, s * GRID : (s + 1) * GRID]], axis=1)
                for s in range(BLOCK)
            ],
            axis=0,
        )
        z = mm(split(stack), wavet)
        lenses = lens_ref[at(i, BLOCK * freqs)]
        lenses = jnp.concatenate(
            [lenses[s * freqs : (s + 1) * freqs] * (2.0 * weight_ref[i * BLOCK + s]) for s in range(BLOCK)], axis=0
        )
        high, less = split(z * jnp.concatenate([lenses, lenses], axis=1))
        place = place_ref[:, at(i, BLOCK * freqs)]
        back_ref[...] += dot(place, high) + dot(place, less)

    each(sources // BLOCK, gradient)

    back = back_ref[...]
    spectrum = split(
        jnp.concatenate(
            [
                jnp.concatenate([back[:HALF, :GRID], -back[:HALF, GRID:]], axis=1),
                jnp.concatenate([back[HALF:, GRID:], back[HALF:, :GRID]], axis=1),
            ],
            axis=0,
        )
    )

    def columns(first_column, count):
        begin = first_column - start
        return mm(pair(across_ref, pl.ds(pl.multiple_of(begin, count), count)), spectrum, NT)

    def give(core, ref, sem):
        offset = pl.multiple_of(jnp.where(edge < 0, 0, width - overlap), overlap)
        return pltpu.make_async_remote_copy(
            src_ref=give_ref,
            dst_ref=ref.at[pl.ds(offset, overlap)],
            send_sem=give_sem.at[sem],
            recv_sem=side_sem.at[sem],
            device_id={"src": taker, "tile": core},
            device_id_type=MESH,
        )

    def take(ref, sem):
        offset = pl.multiple_of(jnp.where(edge < 0, width - overlap, 0), overlap)
        return pltpu.make_async_remote_copy(
            src_ref=give_ref,
            dst_ref=ref.at[pl.ds(offset, overlap)],
            send_sem=give_sem.at[sem],
            recv_sem=side_sem.at[sem],
            device_id={"src": source, "tile": side},
            device_id_type=MESH,
        )

    @pl.when(gives)
    def _():
        give_ref[...] = columns(taker * width + jnp.where(edge < 0, 0, width - overlap), overlap)
        give(side, side_ref, 0).start()
        give(1 - side, corner_ref, 1).start()

    own = columns(me * width, width)
    own_ref[...] = own
    swap = pltpu.make_async_remote_copy(
        src_ref=own_ref,
        dst_ref=other_ref,
        send_sem=own_sem.at[0],
        recv_sem=own_sem.at[1],
        device_id={"tile": 1 - side},
        device_id_type=MESH,
    )
    swap.start()
    downt = pair(downt_ref)
    out_ref[...] = mm(downt, split(own), NT)
    swap.wait_recv()
    out_ref[pl.ds(first, HALO), :] += mm(pair(neart_ref), split(other_ref[...]), NT)

    @pl.when(needs)
    def _():
        take(side_ref, 0).wait_recv()
        out_ref[...] += mm(downt, split(side_ref[...]), NT)
        take(corner_ref, 1).wait_recv()
        out_ref[pl.ds(first, HALO), :] += mm(pair(neart_ref), split(corner_ref[...]), NT)

    @pl.when(gives)
    def _():
        give(side, side_ref, 0).wait_send()
        give(1 - side, corner_ref, 1).wait_send()

    halo.wait_send()
    swap.wait_send()


def shards(mask, target, pupil, source_shift, source_weight):
    n = lax.axis_size("src")
    assert lax.axis_size("tile") == 2
    sources = source_shift.shape[0]
    freqs = pupil.shape[0]
    columns = mask.shape[1]
    tiles = columns // TS
    assert tiles == 2
    width = columns // n
    overlap = min(width, HALO)
    hop = 1 << ((n.bit_length() - 1) // 2)
    across, down, wave, turn, core = tables(freqs)
    local = down[:, HALO : HALO + TS]
    near = np.stack([down[:, HALO + TS :], down[:, :HALO]])
    turn_two = two(turn)
    constants = [
        two(across), two(local), two(local.T),
        np.stack([two(near[0]), two(near[1])]), np.stack([two(near[0].T), two(near[1].T)]),
        two(wave), two(wave.T), np.concatenate([turn_two[0], turn_two[1], turn_two[0]], axis=1), two(turn.T),
        two(core), two(core.T),
    ]
    scratch = [
        (2, PAD, 2 * GRID), (2, GRID, TS), (2, TS, GRID), (2, GRID, HALO), (2, HALO, GRID),
        (2, 2 * GRID, 2 * GRID), (2, 2 * GRID, 2 * GRID), (2 * GRID, 3 * GRID), (2, GRID, 2 * GRID),
        (2, TS, GRID), (2, GRID, TS),
    ]
    hbm = pl.BlockSpec(memory_space=pl.ANY)
    vmem = pl.BlockSpec(memory_space=pltpu.VMEM)
    smem = pl.BlockSpec(memory_space=pltpu.SMEM)
    return pl.pallas_call(
        functools.partial(kernel, n, tiles, sources, freqs, overlap, hop),
        out_shape=jax.ShapeDtypeStruct((TS, width), f32),
        in_specs=[hbm, hbm, vmem, smem, smem] + [hbm] * len(constants),
        out_specs=vmem,
        scratch_shapes=[pltpu.VMEM(shape, bf16) for shape in scratch] + [
            pltpu.VMEM((TS, PAD), f32),
            pltpu.VMEM((TS, TS), f32),
            pltpu.VMEM((HALO, PAD), f32),
            pltpu.VMEM((sources * freqs, GRID), f32),
            pltpu.VMEM((sources * freqs, 2 * GRID), bf16),
            pltpu.VMEM((GRID, sources * freqs), bf16),
            pltpu.VMEM((2 * GRID, sources * GRID), f32),
            pltpu.VMEM((GRID, GRID), f32),
            pltpu.VMEM((GRID, GRID), f32),
            pltpu.VMEM((GRID, 2 * GRID), f32),
            pltpu.VMEM((width, GRID), f32),
            pltpu.VMEM((width, GRID), f32),
            pltpu.VMEM((overlap, GRID), f32),
            pltpu.VMEM((width, GRID), f32),
            pltpu.VMEM((width, GRID), f32),
            pltpu.SemaphoreType.DMA((2 + len(constants),)),
            pltpu.SemaphoreType.DMA((2,)),
            pltpu.SemaphoreType.DMA((2,)),
            pltpu.SemaphoreType.DMA((2,)),
            pltpu.SemaphoreType.DMA((2,)),
        ],
        compiler_params=pltpu.CompilerParams(
            collective_id=0, has_side_effects=True, vmem_limit_bytes=60 * 1024 * 1024
        ),
    )(mask, target, pupil, source_shift.T, source_weight, *[jnp.asarray(x) for x in constants])


def solution(mesh):
    placed = (P(("groups", "tile"), None), P(("groups", "tile"), None), P(), P(), P())
    return jax.shard_map(
        shards, mesh=mesh, in_specs=placed, out_specs=P(("groups", "tile"), "src"), check_vma=False
    )
```

```python
import functools

import numpy as np

import jax
import jax.numpy as jnp
from jax import lax
from jax.experimental import pallas as pl
from jax.experimental.pallas import tpu as pltpu
from jax.sharding import PartitionSpec as P

TS = 512
HALO = 64
PAD = 640
GRID = 128
REACH = 24
HALF = GRID // 2
CHUNK = 128
BLOCK = 24

MESH = pl.DeviceIdType.MESH
f32, bf16 = jnp.float32, jnp.bfloat16
resist_gain = 25.0
resist_level = 0.25

NN = (((1,), (0,)), ((), ()))
NT = (((1,), (1,)), ((), ()))


def two(array):
    high = array.astype(np.float32).astype(bf16)
    low = (array - high.astype(np.float64)).astype(bf16)
    return np.stack([high, low])


def tables(freqs):
    turn_of = 2.0 * np.pi / PAD
    reach = freqs // 2 + REACH
    frame = np.zeros(GRID)
    frame[: 2 * reach] = np.arange(-reach, reach)
    inside = np.zeros(GRID)
    inside[: 2 * reach] = 1.0

    columns = np.arange(-HALO, PAD + HALO)
    angle = turn_of * ((columns[:, None] * frame[None, :].astype(int)) % PAD)
    valid = ((columns >= 0) & (columns < PAD))[:, None] * inside[None, :]
    across = np.concatenate([np.cos(angle) * valid, np.sin(angle) * valid], axis=1)

    rows = np.arange(PAD)
    k = np.arange(HALF)
    used = (k <= reach)[:, None]
    angle = turn_of * ((k[:, None] * rows[None, :]) % PAD)
    down = np.concatenate([np.cos(angle) * used, -np.sin(angle) * used], axis=0)

    points = np.arange(GRID)
    angle = 2.0 * np.pi / GRID * ((frame[:, None].astype(int) * points[None, :]) % GRID)
    cosine, sine = np.cos(angle) * inside[:, None], np.sin(angle) * inside[:, None]
    wave = np.block([[cosine, sine], [-sine, cosine]])

    centre = np.arange(-freqs // 2, freqs // 2)
    angle = 2.0 * np.pi / GRID * ((points[:, None] * centre[None, :]) % GRID)
    turn = np.block([[np.cos(angle), -np.sin(angle)], [np.sin(angle), np.cos(angle)]])

    samples = points * (PAD // GRID)
    spread = np.ones((PAD, GRID))
    for p in range(1, GRID // 2):
        spread += 2.0 * np.cos(2.0 * np.pi * (p * (rows[:, None] - samples[None, :]) % PAD) / PAD)
    core = (spread / GRID)[HALO : HALO + TS]
    unpack = np.zeros((GRID, GRID))
    for i in range(2 * reach):
        w = i - reach
        unpack[i, abs(w)] = 1.0
        unpack[i, HALF + abs(w)] = np.sign(w)
    return across, down, wave, turn, core, unpack


def split(x):
    high = x.astype(bf16)
    return high, (x - high.astype(f32)).astype(bf16)


def dot(a, b, dims=NN):
    return lax.dot_general(a, b, dims, preferred_element_type=f32)


def mm(a, b, dims=NN):
    return dot(a[0], b[0], dims) + (dot(a[0], b[1], dims) + dot(a[1], b[0], dims))


def pair(ref, *index):
    return ref[(0, *index)], ref[(1, *index)]


def each(count, body, most=BLOCK):
    if count <= most:
        for i in range(count):
            body(i)
    else:
        lax.fori_loop(0, count, lambda i, c: (body(i), c)[1], 0)


def at(i, size):
    start = i * size
    return pl.ds(start if isinstance(start, int) else pl.multiple_of(start, size), size)


def kernel(
    n, tiles, sources, freqs, overlap, hop,
    mask_any, target_any, pupil_ref, shift_ref, weight_ref,
    unpack_any, repack_any, across_any, down_any, downt_any, near_any, neart_any, wave_any, wavet_any, turn_any, turnt_any, core_any, coret_any,
    out_ref,
    unpack_ref, repack_ref, across_ref, down_ref, downt_ref, near_ref, neart_ref, wave_ref, wavet_ref, turn_ref, turnt_ref, core_ref, coret_ref,
    mask_ref, target_ref, halo_ref, lens_ref, pick_ref, place_ref, field_ref, light_ref, pull_ref, back_ref,
    own_ref, other_ref, give_ref, side_ref, corner_ref,
    load_sem, halo_sem, own_sem, give_sem, side_sem,
):
    me = lax.axis_index("src")
    side = lax.axis_index("tile")
    per = n // tiles
    c = me // per
    width = out_ref.shape[1]
    counted = HALO // overlap
    edge = me - per
    lefts = (edge >= -counted) & (edge < 0)
    rights = (edge >= 0) & (edge < counted)
    needs = lefts | rights
    source = jnp.where(edge < 0, me + hop, me - hop)
    gives = ((edge - hop >= -counted) & (edge - hop < 0)) | ((edge + hop >= 0) & (edge + hop < counted))
    taker = jnp.where(edge < 0, me + hop, me - hop)

    barrier = pltpu.get_barrier_semaphore()
    side_ref[...] = jnp.zeros_like(side_ref)
    corner_ref[...] = jnp.zeros_like(corner_ref)
    pl.semaphore_signal(barrier, inc=1, device_id={"tile": 1 - side}, device_id_type=MESH)

    @pl.when(needs)
    def _():
        for core in (0, 1):
            pl.semaphore_signal(barrier, inc=1, device_id={"src": source, "tile": core}, device_id_type=MESH)

    first = pl.multiple_of((TS - HALO) * (1 - side), HALO)
    start = pl.multiple_of(c * (mask_any.shape[1] - PAD), GRID)
    begin = pl.multiple_of(c * TS, GRID)
    places = [
        (unpack_any, unpack_ref), (repack_any, repack_ref), (mask_any.at[:, pl.ds(start, PAD)], mask_ref), (down_any, down_ref), (near_any.at[side], near_ref),
        (across_any.at[:, pl.ds(pl.multiple_of((1 - c) * 2 * HALO, GRID), PAD)], across_ref),
        (wave_any, wave_ref), (turn_any, turn_ref), (core_any, core_ref), (coret_any, coret_ref),
        (target_any.at[:, pl.ds(begin, TS)], target_ref), (turnt_any, turnt_ref), (wavet_any, wavet_ref),
        (downt_any, downt_ref), (neart_any.at[1 - side], neart_ref),
    ]
    loads = [pltpu.make_async_copy(a, b, load_sem.at[i]) for i, (a, b) in enumerate(places)]
    for load in loads:
        load.start()

    scaled = jnp.concatenate([pupil_ref[...] * (1.0 / (PAD * PAD)), jnp.zeros((freqs, GRID - freqs), f32)], axis=1)

    for load in loads[:2]:
        load.wait()
    lane = lax.broadcasted_iota(jnp.int32, (GRID, GRID), 1)

    def lens(s):
        lens_ref[at(s, freqs)] = pltpu.roll(scaled, shift_ref[1, s] + REACH, axis=1)
        window = unpack_ref[pl.ds(shift_ref[0, s] + REACH, freqs)].astype(bf16)
        pick_ref[at(s, freqs)] = jnp.concatenate([window, window], axis=1)

    each(sources, lens)

    group = GRID // freqs

    def places_of(i):
        repack = repack_ref[...]
        place = pltpu.roll(repack, GRID - REACH - shift_ref[0, i * group], axis=1)
        for g in range(1, group):
            shift = GRID - REACH + g * freqs - shift_ref[0, i * group + g]
            place = jnp.where(lane >= g * freqs, pltpu.roll(repack, lax.rem(shift, GRID), axis=1), place)
        place_ref[:, at(i, GRID)] = place.astype(bf16)

    each(sources // group, places_of)

    weight = weight_ref[0]
    for s in range(1, sources):
        weight = weight + weight_ref[s]
    inverse = 1.0 / jnp.full((1, GRID), weight, f32)

    pl.semaphore_wait(barrier, 1 + 2 * gives.astype(jnp.int32))
    halo = pltpu.make_async_remote_copy(
        src_ref=mask_any.at[pl.ds(first, HALO), pl.ds(start, PAD)],
        dst_ref=halo_ref,
        send_sem=halo_sem.at[0],
        recv_sem=halo_sem.at[1],
        device_id={"tile": 1 - side},
        device_id_type=MESH,
    )
    halo.start()

    for load in loads[2:5]:
        load.wait()
    rows = mm(pair(down_ref), split(mask_ref[...]))
    halo.wait_recv()
    rows = rows + mm(pair(near_ref), split(halo_ref[...]))
    loads[5].wait()
    low = mm(split(rows), pair(across_ref))
    spectrum = split(
        jnp.concatenate(
            [
                jnp.concatenate([low[:HALF, :GRID], -low[:HALF, GRID:]], axis=1),
                jnp.concatenate([low[HALF:, GRID:], low[HALF:, :GRID]], axis=1),
            ],
            axis=0,
        )
    )
    spectrum = jnp.concatenate(spectrum, axis=0)

    for load in loads[6:8]:
        load.wait()
    light_ref[...] = jnp.zeros_like(light_ref)
    wave = pair(wave_ref)
    turn = turn_ref[...]

    def image(i):
        window = dot(pick_ref[at(i, BLOCK * freqs)], spectrum)
        lenses = lens_ref[at(i, BLOCK * freqs)]
        spec = split(window * jnp.concatenate([lenses, lenses], axis=1))
        z = mm(spec, wave)
        stack = jnp.concatenate(
            [
                jnp.concatenate([z[s * freqs : (s + 1) * freqs, :GRID], z[s * freqs : (s + 1) * freqs, GRID:]], axis=0)
                for s in range(BLOCK)
            ],
            axis=1,
        )
        high, less = split(stack)
        field = dot(turn, jnp.concatenate([high, high, less], axis=0))
        field_ref[:, at(i, BLOCK * GRID)] = field
        light = light_ref[...]
        for s in range(BLOCK):
            re = field[:GRID, s * GRID : (s + 1) * GRID]
            im = field[GRID:, s * GRID : (s + 1) * GRID]
            light = light + weight_ref[i * BLOCK + s] * (re * re + im * im)
        light_ref[...] = light

    each(sources // BLOCK, image, 1)

    for load in loads[8:11]:
        load.wait()
    core = pair(core_ref)
    coret = pair(coret_ref)
    up = mm(core, split(light_ref[...] * (resist_gain * inverse)))
    pull = jnp.zeros((GRID, GRID), f32)
    for i in range(TS // CHUNK):
        part = slice(i * CHUNK, (i + 1) * CHUNK)
        fine = mm(split(up[part]), coret)
        decay = jnp.exp(resist_gain * resist_level - fine)
        printed = 1.0 / (1.0 + decay)
        slope = (printed - target_ref[part]) * (decay * printed * printed)
        pull = pull + mm(pair(coret_ref, slice(None), part), split(mm(split(slope), core)))
    pull = pull * (2.0 * resist_gain * inverse)
    pull = jnp.concatenate([pull, pull], axis=0)

    for load in loads[11:]:
        load.wait()
    turnt = pair(turnt_ref)
    wavet = pair(wavet_ref)
    back_ref[...] = jnp.zeros_like(back_ref)

    def gradient(i):
        field = field_ref[:, at(i, BLOCK * GRID)]
        u = mm(turnt, split(field * jnp.concatenate([pull] * BLOCK, axis=1)))
        stack = jnp.concatenate(
            [
                jnp.concatenate([u[:freqs, s * GRID : (s + 1) * GRID], u[freqs:, s * GRID : (s + 1) * GRID]], axis=1)
                for s in range(BLOCK)
            ],
            axis=0,
        )
        z = mm(split(stack), wavet)
        lenses = lens_ref[at(i, BLOCK * freqs)]
        lenses = jnp.concatenate(
            [lenses[s * freqs : (s + 1) * freqs] * (2.0 * weight_ref[i * BLOCK + s]) for s in range(BLOCK)], axis=0
        )
        high, less = split(z * jnp.concatenate([lenses, lenses], axis=1))
        place = place_ref[:, at(i, BLOCK * freqs)]
        back_ref[...] += dot(place, high) + dot(place, less)

    each(sources // BLOCK, gradient, 1)

    back = back_ref[...]
    spectrum = split(
        jnp.concatenate(
            [
                jnp.concatenate([back[:HALF, :GRID], -back[:HALF, GRID:]], axis=1),
                jnp.concatenate([back[HALF:, GRID:], back[HALF:, :GRID]], axis=1),
            ],
            axis=0,
        )
    )

    def columns(first_column, count):
        begin = first_column - start
        return mm(pair(across_ref, pl.ds(pl.multiple_of(begin, count), count)), spectrum, NT)

    def give(core, ref, sem):
        offset = pl.multiple_of(jnp.where(edge < 0, 0, width - overlap), overlap)
        return pltpu.make_async_remote_copy(
            src_ref=give_ref,
            dst_ref=ref.at[pl.ds(offset, overlap)],
            send_sem=give_sem.at[sem],
            recv_sem=side_sem.at[sem],
            device_id={"src": taker, "tile": core},
            device_id_type=MESH,
        )

    def take(ref, sem):
        offset = pl.multiple_of(jnp.where(edge < 0, width - overlap, 0), overlap)
        return pltpu.make_async_remote_copy(
            src_ref=give_ref,
            dst_ref=ref.at[pl.ds(offset, overlap)],
            send_sem=give_sem.at[sem],
            recv_sem=side_sem.at[sem],
            device_id={"src": source, "tile": side},
            device_id_type=MESH,
        )

    @pl.when(gives)
    def _():
        give_ref[...] = columns(taker * width + jnp.where(edge < 0, 0, width - overlap), overlap)
        give(side, side_ref, 0).start()
        give(1 - side, corner_ref, 1).start()

    own = columns(me * width, width)
    own_ref[...] = own
    swap = pltpu.make_async_remote_copy(
        src_ref=own_ref,
        dst_ref=other_ref,
        send_sem=own_sem.at[0],
        recv_sem=own_sem.at[1],
        device_id={"tile": 1 - side},
        device_id_type=MESH,
    )
    swap.start()
    downt = pair(downt_ref)
    out_ref[...] = mm(downt, split(own), NT)
    swap.wait_recv()
    out_ref[pl.ds(first, HALO), :] += mm(pair(neart_ref), split(other_ref[...]), NT)

    @pl.when(needs)
    def _():
        take(side_ref, 0).wait_recv()
        out_ref[...] += mm(downt, split(side_ref[...]), NT)
        take(corner_ref, 1).wait_recv()
        out_ref[pl.ds(first, HALO), :] += mm(pair(neart_ref), split(corner_ref[...]), NT)

    @pl.when(gives)
    def _():
        give(side, side_ref, 0).wait_send()
        give(1 - side, corner_ref, 1).wait_send()

    halo.wait_send()
    swap.wait_send()


def shards(mask, target, pupil, source_shift, source_weight):
    n = lax.axis_size("src")
    assert lax.axis_size("tile") == 2
    sources = source_shift.shape[0]
    freqs = pupil.shape[0]
    columns = mask.shape[1]
    tiles = columns // TS
    assert tiles == 2
    width = columns // n
    overlap = min(width, HALO)
    hop = 1 << ((n.bit_length() - 1) // 2)
    across, down, wave, turn, core, unpack = tables(freqs)
    local = down[:, HALO : HALO + TS]
    near = np.stack([down[:, HALO + TS :], down[:, :HALO]])
    turn_two = two(turn)
    constants = [
        unpack.astype(np.float32), unpack.T.astype(np.float32), two(across), two(local), two(local.T),
        np.stack([two(near[0]), two(near[1])]), np.stack([two(near[0].T), two(near[1].T)]),
        two(wave), two(wave.T), np.concatenate([turn_two[0], turn_two[1], turn_two[0]], axis=1), two(turn.T),
        two(core), two(core.T),
    ]
    scratch = [
        (2, PAD, 2 * GRID), (2, GRID, TS), (2, TS, GRID), (2, GRID, HALO), (2, HALO, GRID),
        (2, 2 * GRID, 2 * GRID), (2, 2 * GRID, 2 * GRID), (2 * GRID, 3 * GRID), (2, GRID, 2 * GRID),
        (2, TS, GRID), (2, GRID, TS),
    ]
    hbm = pl.BlockSpec(memory_space=pl.ANY)
    vmem = pl.BlockSpec(memory_space=pltpu.VMEM)
    smem = pl.BlockSpec(memory_space=pltpu.SMEM)
    return pl.pallas_call(
        functools.partial(kernel, n, tiles, sources, freqs, overlap, hop),
        out_shape=jax.ShapeDtypeStruct((TS, width), f32),
        in_specs=[hbm, hbm, vmem, smem, smem] + [hbm] * len(constants),
        out_specs=vmem,
        scratch_shapes=[pltpu.VMEM((GRID, GRID), f32)] * 2 + [pltpu.VMEM(shape, bf16) for shape in scratch] + [
            pltpu.VMEM((TS, PAD), f32),
            pltpu.VMEM((TS, TS), f32),
            pltpu.VMEM((HALO, PAD), f32),
            pltpu.VMEM((sources * freqs, GRID), f32),
            pltpu.VMEM((sources * freqs, 2 * GRID), bf16),
            pltpu.VMEM((GRID, sources * freqs), bf16),
            pltpu.VMEM((2 * GRID, sources * GRID), f32),
            pltpu.VMEM((GRID, GRID), f32),
            pltpu.VMEM((GRID, GRID), f32),
            pltpu.VMEM((GRID, 2 * GRID), f32),
            pltpu.VMEM((width, GRID), f32),
            pltpu.VMEM((width, GRID), f32),
            pltpu.VMEM((overlap, GRID), f32),
            pltpu.VMEM((width, GRID), f32),
            pltpu.VMEM((width, GRID), f32),
            pltpu.SemaphoreType.DMA((2 + len(constants),)),
            pltpu.SemaphoreType.DMA((2,)),
            pltpu.SemaphoreType.DMA((2,)),
            pltpu.SemaphoreType.DMA((2,)),
            pltpu.SemaphoreType.DMA((2,)),
        ],
        compiler_params=pltpu.CompilerParams(
            collective_id=0, has_side_effects=True, vmem_limit_bytes=60 * 1024 * 1024
        ),
    )(mask, target, pupil, source_shift.T, source_weight, *[jnp.asarray(x) for x in constants])


def solution(mesh):
    placed = (P(("groups", "tile"), None), P(("groups", "tile"), None), P(), P(), P())
    return jax.shard_map(
        shards, mesh=mesh, in_specs=placed, out_specs=P(("groups", "tile"), "src"), check_vma=False
    )
```

```python
import functools

import numpy as np

import jax
import jax.numpy as jnp
from jax import lax
from jax.experimental import pallas as pl
from jax.experimental.pallas import tpu as pltpu
from jax.sharding import PartitionSpec as P

TS = 512
HALO = 64
PAD = 640
GRID = 128
REACH = 24
HALF = GRID // 2
CHUNK = 256
BLOCK = 24

MESH = pl.DeviceIdType.MESH
f32, bf16 = jnp.float32, jnp.bfloat16
resist_gain = 25.0
resist_level = 0.25

NN = (((1,), (0,)), ((), ()))
NT = (((1,), (1,)), ((), ()))


def two(array):
    high = array.astype(np.float32).astype(bf16)
    low = (array - high.astype(np.float64)).astype(bf16)
    return np.stack([high, low])


def tables(freqs):
    turn_of = 2.0 * np.pi / PAD
    reach = freqs // 2 + REACH
    frame = np.zeros(GRID)
    frame[: 2 * reach] = np.arange(-reach, reach)
    inside = np.zeros(GRID)
    inside[: 2 * reach] = 1.0

    columns = np.arange(-HALO, PAD + HALO)
    angle = turn_of * ((columns[:, None] * frame[None, :].astype(int)) % PAD)
    valid = ((columns >= 0) & (columns < PAD))[:, None] * inside[None, :]
    across = np.concatenate([np.cos(angle) * valid, np.sin(angle) * valid], axis=1)

    rows = np.arange(PAD)
    k = np.arange(HALF)
    used = (k <= reach)[:, None]
    angle = turn_of * ((k[:, None] * rows[None, :]) % PAD)
    down = np.concatenate([np.cos(angle) * used, -np.sin(angle) * used], axis=0)

    points = np.arange(GRID)
    angle = 2.0 * np.pi / GRID * ((frame[:, None].astype(int) * points[None, :]) % GRID)
    cosine, sine = np.cos(angle) * inside[:, None], np.sin(angle) * inside[:, None]
    wave = np.block([[cosine, sine], [-sine, cosine]])

    centre = np.arange(-freqs // 2, freqs // 2)
    angle = 2.0 * np.pi / GRID * ((points[:, None] * centre[None, :]) % GRID)
    turn = np.block([[np.cos(angle), -np.sin(angle)], [np.sin(angle), np.cos(angle)]])

    samples = points * (PAD // GRID)
    spread = np.ones((PAD, GRID))
    for p in range(1, GRID // 2):
        spread += 2.0 * np.cos(2.0 * np.pi * (p * (rows[:, None] - samples[None, :]) % PAD) / PAD)
    core = (spread / GRID)[HALO : HALO + TS]
    unpack = np.zeros((GRID, GRID))
    for i in range(2 * reach):
        w = i - reach
        unpack[i, abs(w)] = 1.0
        unpack[i, HALF + abs(w)] = np.sign(w)
    return across, down, wave, turn, core, unpack


def split(x):
    high = x.astype(bf16)
    return high, (x - high.astype(f32)).astype(bf16)


def dot(a, b, dims=NN):
    return lax.dot_general(a, b, dims, preferred_element_type=f32)


def mm(a, b, dims=NN):
    axis = dims[0][1][0]
    return dot(jnp.concatenate([a[0], a[0], a[1]], axis=1), jnp.concatenate([b[0], b[1], b[0]], axis=axis), dims)


def pair(ref, *index):
    return ref[(0, *index)], ref[(1, *index)]


def each(count, body, most=BLOCK):
    if count <= most:
        for i in range(count):
            body(i)
    else:
        lax.fori_loop(0, count, lambda i, c: (body(i), c)[1], 0)


def at(i, size):
    start = i * size
    return pl.ds(start if isinstance(start, int) else pl.multiple_of(start, size), size)


def kernel(
    n, tiles, sources, freqs, overlap, hop,
    mask_any, target_any, pupil_ref, shift_ref, weight_ref,
    unpack_any, repack_any, across_any, down_any, downt_any, near_any, neart_any, wave_any, wavet_any, turn_any, turnt_any, core_any, coret_any,
    out_ref,
    unpack_ref, repack_ref, across_ref, down_ref, downt_ref, near_ref, neart_ref, wave_ref, wavet_ref, turn_ref, turnt_ref, core_ref, coret_ref,
    mask_ref, target_ref, halo_ref, lens_ref, pick_ref, place_ref, field_ref, light_ref, pull_ref, back_ref,
    own_ref, other_ref, give_ref, side_ref, corner_ref,
    load_sem, halo_sem, own_sem, give_sem, side_sem,
):
    me = lax.axis_index("src")
    side = lax.axis_index("tile")
    per = n // tiles
    c = me // per
    width = out_ref.shape[1]
    counted = HALO // overlap
    edge = me - per
    lefts = (edge >= -counted) & (edge < 0)
    rights = (edge >= 0) & (edge < counted)
    needs = lefts | rights
    source = jnp.where(edge < 0, me + hop, me - hop)
    gives = ((edge - hop >= -counted) & (edge - hop < 0)) | ((edge + hop >= 0) & (edge + hop < counted))
    taker = jnp.where(edge < 0, me + hop, me - hop)

    barrier = pltpu.get_barrier_semaphore()
    side_ref[...] = jnp.zeros_like(side_ref)
    corner_ref[...] = jnp.zeros_like(corner_ref)
    pl.semaphore_signal(barrier, inc=1, device_id={"tile": 1 - side}, device_id_type=MESH)

    @pl.when(needs)
    def _():
        for core in (0, 1):
            pl.semaphore_signal(barrier, inc=1, device_id={"src": source, "tile": core}, device_id_type=MESH)

    first = pl.multiple_of((TS - HALO) * (1 - side), HALO)
    start = pl.multiple_of(c * (mask_any.shape[1] - PAD), GRID)
    begin = pl.multiple_of(c * TS, GRID)
    places = [
        (unpack_any, unpack_ref), (repack_any, repack_ref), (mask_any.at[:, pl.ds(start, PAD)], mask_ref), (down_any, down_ref), (near_any.at[side], near_ref),
        (across_any.at[:, pl.ds(pl.multiple_of((1 - c) * 2 * HALO, GRID), PAD)], across_ref),
        (wave_any, wave_ref), (turn_any, turn_ref), (core_any, core_ref), (coret_any, coret_ref),
        (target_any.at[:, pl.ds(begin, TS)], target_ref), (turnt_any, turnt_ref), (wavet_any, wavet_ref),
        (downt_any, downt_ref), (neart_any.at[1 - side], neart_ref),
    ]
    loads = [pltpu.make_async_copy(a, b, load_sem.at[i]) for i, (a, b) in enumerate(places)]
    for load in loads:
        load.start()

    scaled = jnp.concatenate([pupil_ref[...] * (1.0 / (PAD * PAD)), jnp.zeros((freqs, GRID - freqs), f32)], axis=1)

    for load in loads[:2]:
        load.wait()
    lane = lax.broadcasted_iota(jnp.int32, (GRID, GRID), 1)

    def lens(s):
        lens_ref[at(s, freqs)] = pltpu.roll(scaled, shift_ref[1, s] + REACH, axis=1)
        window = unpack_ref[pl.ds(shift_ref[0, s] + REACH, freqs)].astype(bf16)
        pick_ref[at(s, freqs)] = jnp.concatenate([window, window], axis=1)

    each(sources, lens)

    group = GRID // freqs

    def places_of(i):
        repack = repack_ref[...]
        place = pltpu.roll(repack, GRID - REACH - shift_ref[0, i * group], axis=1)
        for g in range(1, group):
            shift = GRID - REACH + g * freqs - shift_ref[0, i * group + g]
            place = jnp.where(lane >= g * freqs, pltpu.roll(repack, lax.rem(shift, GRID), axis=1), place)
        place_ref[:, at(i, GRID)] = place.astype(bf16)

    each(sources // group, places_of)

    weight = weight_ref[0]
    for s in range(1, sources):
        weight = weight + weight_ref[s]
    inverse = 1.0 / jnp.full((1, GRID), weight, f32)

    pl.semaphore_wait(barrier, 1 + 2 * gives.astype(jnp.int32))
    halo = pltpu.make_async_remote_copy(
        src_ref=mask_any.at[pl.ds(first, HALO), pl.ds(start, PAD)],
        dst_ref=halo_ref,
        send_sem=halo_sem.at[0],
        recv_sem=halo_sem.at[1],
        device_id={"tile": 1 - side},
        device_id_type=MESH,
    )
    halo.start()

    for load in loads[2:5]:
        load.wait()
    rows = mm(pair(down_ref), split(mask_ref[...]))
    halo.wait_recv()
    rows = rows + mm(pair(near_ref), split(halo_ref[...]))
    loads[5].wait()
    low = mm(split(rows), pair(across_ref))
    spectrum = split(
        jnp.concatenate(
            [
                jnp.concatenate([low[:HALF, :GRID], -low[:HALF, GRID:]], axis=1),
                jnp.concatenate([low[HALF:, GRID:], low[HALF:, :GRID]], axis=1),
            ],
            axis=0,
        )
    )
    spectrum = jnp.concatenate(spectrum, axis=0)

    for load in loads[6:8]:
        load.wait()
    light_ref[...] = jnp.zeros_like(light_ref)
    wave = pair(wave_ref)
    turn = turn_ref[...]

    def image(i):
        window = dot(pick_ref[at(i, BLOCK * freqs)], spectrum)
        lenses = lens_ref[at(i, BLOCK * freqs)]
        spec = split(window * jnp.concatenate([lenses, lenses], axis=1))
        z = mm(spec, wave)
        stack = jnp.concatenate(
            [
                jnp.concatenate([z[s * freqs : (s + 1) * freqs, :GRID], z[s * freqs : (s + 1) * freqs, GRID:]], axis=0)
                for s in range(BLOCK)
            ],
            axis=1,
        )
        high, less = split(stack)
        field = dot(turn, jnp.concatenate([high, high, less], axis=0))
        field_ref[:, at(i, BLOCK * GRID)] = field
        light = light_ref[...]
        for s in range(BLOCK):
            re = field[:GRID, s * GRID : (s + 1) * GRID]
            im = field[GRID:, s * GRID : (s + 1) * GRID]
            light = light + weight_ref[i * BLOCK + s] * (re * re + im * im)
        light_ref[...] = light

    each(sources // BLOCK, image, 1)

    for load in loads[8:11]:
        load.wait()
    core = pair(core_ref)
    coret = pair(coret_ref)
    up = mm(core, split(light_ref[...] * (resist_gain * inverse)))
    pull = jnp.zeros((GRID, GRID), f32)
    for i in range(TS // CHUNK):
        part = slice(i * CHUNK, (i + 1) * CHUNK)
        fine = mm(split(up[part]), coret)
        decay = jnp.exp(resist_gain * resist_level - fine)
        printed = 1.0 / (1.0 + decay)
        slope = (printed - target_ref[part]) * (decay * printed * printed)
        pull = pull + mm(pair(coret_ref, slice(None), part), split(mm(split(slope), core)))
    pull = pull * (2.0 * resist_gain * inverse)
    pull = jnp.concatenate([pull, pull], axis=0)

    for load in loads[11:]:
        load.wait()
    turnt = pair(turnt_ref)
    wavet = pair(wavet_ref)
    back_ref[...] = jnp.zeros_like(back_ref)

    def gradient(i):
        field = field_ref[:, at(i, BLOCK * GRID)]
        u = mm(turnt, split(field * jnp.concatenate([pull] * BLOCK, axis=1)))
        stack = jnp.concatenate(
            [
                jnp.concatenate([u[:freqs, s * GRID : (s + 1) * GRID], u[freqs:, s * GRID : (s + 1) * GRID]], axis=1)
                for s in range(BLOCK)
            ],
            axis=0,
        )
        z = mm(split(stack), wavet)
        lenses = lens_ref[at(i, BLOCK * freqs)]
        lenses = jnp.concatenate(
            [lenses[s * freqs : (s + 1) * freqs] * (2.0 * weight_ref[i * BLOCK + s]) for s in range(BLOCK)], axis=0
        )
        high, less = split(z * jnp.concatenate([lenses, lenses], axis=1))
        place = place_ref[:, at(i, BLOCK * freqs)]
        back_ref[...] += dot(place, high) + dot(place, less)

    each(sources // BLOCK, gradient, 1)

    back = back_ref[...]
    spectrum = split(
        jnp.concatenate(
            [
                jnp.concatenate([back[:HALF, :GRID], -back[:HALF, GRID:]], axis=1),
                jnp.concatenate([back[HALF:, GRID:], back[HALF:, :GRID]], axis=1),
            ],
            axis=0,
        )
    )

    def columns(first_column, count):
        begin = first_column - start
        return mm(pair(across_ref, pl.ds(pl.multiple_of(begin, count), count)), spectrum, NT)

    def give(core, ref, sem):
        offset = pl.multiple_of(jnp.where(edge < 0, 0, width - overlap), overlap)
        return pltpu.make_async_remote_copy(
            src_ref=give_ref,
            dst_ref=ref.at[pl.ds(offset, overlap)],
            send_sem=give_sem.at[sem],
            recv_sem=side_sem.at[sem],
            device_id={"src": taker, "tile": core},
            device_id_type=MESH,
        )

    def take(ref, sem):
        offset = pl.multiple_of(jnp.where(edge < 0, width - overlap, 0), overlap)
        return pltpu.make_async_remote_copy(
            src_ref=give_ref,
            dst_ref=ref.at[pl.ds(offset, overlap)],
            send_sem=give_sem.at[sem],
            recv_sem=side_sem.at[sem],
            device_id={"src": source, "tile": side},
            device_id_type=MESH,
        )

    @pl.when(gives)
    def _():
        give_ref[...] = columns(taker * width + jnp.where(edge < 0, 0, width - overlap), overlap)
        give(side, side_ref, 0).start()
        give(1 - side, corner_ref, 1).start()

    own = columns(me * width, width)
    own_ref[...] = own
    swap = pltpu.make_async_remote_copy(
        src_ref=own_ref,
        dst_ref=other_ref,
        send_sem=own_sem.at[0],
        recv_sem=own_sem.at[1],
        device_id={"tile": 1 - side},
        device_id_type=MESH,
    )
    swap.start()
    downt = pair(downt_ref)
    out_ref[...] = mm(downt, split(own), NT)
    swap.wait_recv()
    out_ref[pl.ds(first, HALO), :] += mm(pair(neart_ref), split(other_ref[...]), NT)

    @pl.when(needs)
    def _():
        take(side_ref, 0).wait_recv()
        out_ref[...] += mm(downt, split(side_ref[...]), NT)
        take(corner_ref, 1).wait_recv()
        out_ref[pl.ds(first, HALO), :] += mm(pair(neart_ref), split(corner_ref[...]), NT)

    @pl.when(gives)
    def _():
        give(side, side_ref, 0).wait_send()
        give(1 - side, corner_ref, 1).wait_send()

    halo.wait_send()
    swap.wait_send()


def shards(mask, target, pupil, source_shift, source_weight):
    n = lax.axis_size("src")
    assert lax.axis_size("tile") == 2
    sources = source_shift.shape[0]
    freqs = pupil.shape[0]
    columns = mask.shape[1]
    tiles = columns // TS
    assert tiles == 2
    width = columns // n
    overlap = min(width, HALO)
    hop = 1 << ((n.bit_length() - 1) // 2)
    across, down, wave, turn, core, unpack = tables(freqs)
    local = down[:, HALO : HALO + TS]
    near = np.stack([down[:, HALO + TS :], down[:, :HALO]])
    turn_two = two(turn)
    constants = [
        unpack.astype(np.float32), unpack.T.astype(np.float32), two(across), two(local), two(local.T),
        np.stack([two(near[0]), two(near[1])]), np.stack([two(near[0].T), two(near[1].T)]),
        two(wave), two(wave.T), np.concatenate([turn_two[0], turn_two[1], turn_two[0]], axis=1), two(turn.T),
        two(core), two(core.T),
    ]
    scratch = [
        (2, PAD, 2 * GRID), (2, GRID, TS), (2, TS, GRID), (2, GRID, HALO), (2, HALO, GRID),
        (2, 2 * GRID, 2 * GRID), (2, 2 * GRID, 2 * GRID), (2 * GRID, 3 * GRID), (2, GRID, 2 * GRID),
        (2, TS, GRID), (2, GRID, TS),
    ]
    hbm = pl.BlockSpec(memory_space=pl.ANY)
    vmem = pl.BlockSpec(memory_space=pltpu.VMEM)
    smem = pl.BlockSpec(memory_space=pltpu.SMEM)
    return pl.pallas_call(
        functools.partial(kernel, n, tiles, sources, freqs, overlap, hop),
        out_shape=jax.ShapeDtypeStruct((TS, width), f32),
        in_specs=[hbm, hbm, vmem, smem, smem] + [hbm] * len(constants),
        out_specs=vmem,
        scratch_shapes=[pltpu.VMEM((GRID, GRID), f32)] * 2 + [pltpu.VMEM(shape, bf16) for shape in scratch] + [
            pltpu.VMEM((TS, PAD), f32),
            pltpu.VMEM((TS, TS), f32),
            pltpu.VMEM((HALO, PAD), f32),
            pltpu.VMEM((sources * freqs, GRID), f32),
            pltpu.VMEM((sources * freqs, 2 * GRID), bf16),
            pltpu.VMEM((GRID, sources * freqs), bf16),
            pltpu.VMEM((2 * GRID, sources * GRID), f32),
            pltpu.VMEM((GRID, GRID), f32),
            pltpu.VMEM((GRID, GRID), f32),
            pltpu.VMEM((GRID, 2 * GRID), f32),
            pltpu.VMEM((width, GRID), f32),
            pltpu.VMEM((width, GRID), f32),
            pltpu.VMEM((overlap, GRID), f32),
            pltpu.VMEM((width, GRID), f32),
            pltpu.VMEM((width, GRID), f32),
            pltpu.SemaphoreType.DMA((2 + len(constants),)),
            pltpu.SemaphoreType.DMA((2,)),
            pltpu.SemaphoreType.DMA((2,)),
            pltpu.SemaphoreType.DMA((2,)),
            pltpu.SemaphoreType.DMA((2,)),
        ],
        compiler_params=pltpu.CompilerParams(
            collective_id=0, has_side_effects=True, vmem_limit_bytes=60 * 1024 * 1024
        ),
    )(mask, target, pupil, source_shift.T, source_weight, *[jnp.asarray(x) for x in constants])


def solution(mesh):
    placed = (P(("groups", "tile"), None), P(("groups", "tile"), None), P(), P(), P())
    return jax.shard_map(
        shards, mesh=mesh, in_specs=placed, out_specs=P(("groups", "tile"), "src"), check_vma=False
    )
```
